256 devices in a mesh: segment: 8 (over x, core), seq: 32 (over z, y).
Axes of the slice: x: 4, y: 4, z: 8, core: 2. Of those that a mesh axis runs over, the one named last changes fastest.
Arguments:
- latent: bfloat16 [12288, 1536], P('seq'), may hold values from -4 to 4
- stale_kv: bfloat16 [8, 2, 12288, 1536], P('segment', None, 'seq'), may hold values from -3 to 3
- query_weight: bfloat16 [8, 1536, 1536], P('segment', 'seq'), may hold values from -0.15625 to 0.15625
- key_weight: bfloat16 [8, 1536, 1536], P('segment', 'seq'), may hold values from -0.15625 to 0.15625
- value_weight: bfloat16 [8, 1536, 1536], P('segment', 'seq'), may hold values from -0.15625 to 0.15625
- out_weight: bfloat16 [8, 1536, 1536], P('segment', 'seq'), may hold values from -0.3125 to 0.3125
- query_gain: float32 [8, 128], P('segment'), may hold values from 0.5 to 2
- key_gain: float32 [8, 128], P('segment'), may hold values from 0.5 to 2
- tile_mask: int32 [192, 6], P('seq'), may hold values from -1 to 191, as said below
Outputs:
- section_out: bfloat16 [8, 12288, 1536], P('segment', 'seq')
The draws below stay inside these ranges and needn't reach their ends.
Inputs may be any that keep to these rules, and one draw needn't show every extreme that they name: `tile_mask`: row g lists the key tiles of query tile g: slot 0 holds g itself, the next slots distinct other tiles whose tile-frame (tile number // 6) differs from that of g by at most one, and the remaining slots -1. Every row lists two or more tiles, and some row lists 6.
All inputs are finite; a program needn't handle non-finite values.
Results may differ from the reference program's by a relative error of at most 0.027.
Values may be sent and summed in bfloat16 or wider, within the bound.
No kernel may reach another device: no remote copies, remote signals or barrier semaphores. Data moves between devices by JAX's collectives and lax.ppermute only.
A program may use at most 128 MiB of HBM per device.

```python
import math
import jax
import jax.numpy as jnp
from jax import lax

D = 1536
HEADS = 12
HEAD = 128
TILE = 64
KT = 6
PATCHES = 3
TPP = 2
TPD = 6
NTILES = 192
TOKENS = 12288
N_SEGMENT = 8
N_SEQ = 32


def draw_tile_mask(key, part):
    key_score, key_count = jax.random.split(key)
    query = jnp.arange(NTILES, dtype=jnp.int32)
    frame_of = query // TPD
    candidate = jnp.arange(3 * TPD, dtype=jnp.int32)
    tile_ids = (frame_of[:, None] - 1) * TPD + candidate[None, :]
    allowed = (tile_ids >= 0) & (tile_ids < NTILES) & (tile_ids != query[:, None])
    scores = jax.random.randint(key_score, (NTILES, 3 * TPD), 0, 1 << 20, dtype=jnp.int32) * 256 + candidate[None, :]
    scores = jnp.where(allowed, scores, -1)
    unused, picks = lax.top_k(scores, KT - 1)
    chosen = jnp.take_along_axis(tile_ids, picks, axis=1)
    counts = jax.random.randint(key_count, (NTILES,), 2, KT + 1, dtype=jnp.int32)
    counts = counts.at[0].set(KT).at[1].set(2)
    listed = jnp.concatenate([query[:, None], chosen], axis=1)
    slots = jnp.arange(KT, dtype=jnp.int32)
    return jnp.where(slots[None, :] < counts[:, None], listed, -1).astype(jnp.int32)


def level_of(key, shape, cuts, smallest, largest):
    level = 1.0
    for dim, blocks in cuts:
        draws = jax.random.uniform(jax.random.fold_in(jax.random.fold_in(key, 6), dim), (blocks,), jnp.float32, smallest / len(cuts), largest / len(cuts))
        level = level * jnp.repeat(jnp.exp(draws), shape[dim] // blocks).reshape((-1,) + (1,) * (len(shape) - 1 - dim))
    return level


def bell_draw(own_key, shape, scale, most, shards=(), kind=jnp.bfloat16):
    drawn = scale * jax.random.normal(own_key, shape, jnp.float32)
    if shards:
        drawn = drawn * level_of(own_key, shape, shards, -0.22, 0.18)
    return jnp.clip(drawn, -most, most).astype(kind)


def setup_inputs(seed: int = 0) -> dict:
    key_of = jax.random.split(jax.random.key(seed), 10)
    return {
        "latent": bell_draw(key_of[0], (TOKENS, D), 1.0, 4.0, ((0, 32),)),
        "stale_kv": bell_draw(key_of[1], (N_SEGMENT, 2, TOKENS, D), 1.0, 3.0, ((0, 8), (2, 32))),
        "query_weight": bell_draw(key_of[2], (N_SEGMENT, D, D), D ** -0.5, 0.15625, ((0, 8), (1, 32))),
        "key_weight": bell_draw(key_of[3], (N_SEGMENT, D, D), D ** -0.5, 0.15625, ((0, 8), (1, 32))),
        "value_weight": bell_draw(key_of[4], (N_SEGMENT, D, D), D ** -0.5, 0.15625, ((0, 8), (1, 32))),
        "out_weight": bell_draw(key_of[5], (N_SEGMENT, D, D), (2.0 / D ** 0.5), 0.3125, ((0, 8), (1, 32))),
        "query_gain": jnp.clip(jnp.exp(math.log(2.0) - 1.3862944 * jax.random.uniform(key_of[6], (N_SEGMENT, HEAD), jnp.float32) ** level_of(key_of[6], (N_SEGMENT, HEAD), ((0, 8),), -0.2, 0.2)), 0.5, 2.0),
        "key_gain": jnp.clip(jnp.exp(math.log(2.0) - 1.3862944 * jax.random.uniform(key_of[7], (N_SEGMENT, HEAD), jnp.float32) ** level_of(key_of[7], (N_SEGMENT, HEAD), ((0, 8),), -0.2, 0.2)), 0.5, 2.0),
        "tile_mask": draw_tile_mask(jax.random.fold_in(key_of[9], 71), 0),
    }


epsilon = 1e-06

def head_normed(projected, gain):
    n_rows = projected.shape[0]
    heads = projected.reshape(n_rows, HEADS, HEAD)
    scaled = heads * lax.rsqrt(lax.optimization_barrier(jnp.mean(heads * heads, axis=-1, keepdims=True)) + epsilon)
    return (scaled * gain).reshape(n_rows, D).astype(jnp.bfloat16)

def attend(queries, tile_blocks, tile_lists):
    usable = tile_lists >= 0
    tile_index = jnp.where(usable, tile_lists, 0).astype(jnp.int32)
    n_query = tile_lists.shape[0]
    key_heads = tile_blocks[0][tile_index].astype(jnp.float32).reshape(n_query, KT * TILE, HEADS, HEAD)
    value_heads = tile_blocks[1][tile_index].astype(jnp.float32).reshape(n_query, KT * TILE, HEADS, HEAD)
    query_heads = queries.astype(jnp.float32).reshape(n_query, TILE, HEADS, HEAD)
    scores = jnp.einsum('pthe,pkhe->phtk', query_heads, key_heads) / math.sqrt(HEAD)
    listed = jnp.repeat(usable, TILE, axis=1).astype(jnp.float32)
    weights = jnp.exp(scores) * listed[:, None, None, :]
    totals = lax.optimization_barrier(jnp.sum(weights, axis=-1))
    rounded = lax.optimization_barrier(weights.astype(jnp.bfloat16)).astype(jnp.float32)
    summed = jnp.einsum('phtk,pkhe->pthe', rounded, value_heads)
    return summed / jnp.swapaxes(totals, 1, 2)[..., None]

def reference(latent, stale_kv, query_weight, key_weight, value_weight, out_weight, query_gain, key_gain, tile_mask):
    patch_rows = TPP * TILE
    current = latent.reshape(N_SEQ, PATCHES, patch_rows, D)
    lists_all = tile_mask.reshape(N_SEQ, PATCHES, TPP, KT)
    results = []
    for section in range(N_SEGMENT):
        kv_cache = stale_kv[section].reshape(2, N_SEQ, PATCHES, patch_rows, D)
        produced = jnp.zeros_like(current)
        for patch_id in range(PATCHES):
            inputs = current[:, patch_id].reshape(N_SEQ * patch_rows, D)
            fresh_q = head_normed(jnp.dot(inputs, query_weight[section], preferred_element_type=jnp.float32), query_gain[section])
            fresh_k = head_normed(jnp.dot(inputs, key_weight[section], preferred_element_type=jnp.float32), key_gain[section])
            fresh_v = jnp.dot(inputs, value_weight[section], preferred_element_type=jnp.float32).astype(jnp.bfloat16)
            kv_cache = kv_cache.at[0, :, patch_id].set(fresh_k.reshape(N_SEQ, patch_rows, D))
            kv_cache = kv_cache.at[1, :, patch_id].set(fresh_v.reshape(N_SEQ, patch_rows, D))
            tile_blocks = kv_cache.reshape(2, NTILES, TILE, D)
            tile_lists = lists_all[:, patch_id].reshape(N_SEQ * TPP, KT)
            attention = attend(fresh_q.reshape(N_SEQ * TPP, TILE, D), tile_blocks, tile_lists)
            attention_b = attention.reshape(N_SEQ * patch_rows, D).astype(jnp.bfloat16)
            mixed = jnp.dot(attention_b, out_weight[section], preferred_element_type=jnp.float32)
            leaving = (inputs.astype(jnp.float32) + mixed).astype(jnp.bfloat16)
            produced = produced.at[:, patch_id].set(leaving.reshape(N_SEQ, patch_rows, D))
        results.append(produced.reshape(TOKENS, D))
        current = produced
    return jnp.stack(results)
```

```python
import functools
import math

import jax
import jax.numpy as jnp
from jax import lax
from jax.experimental import pallas as pl
from jax.experimental.pallas import tpu as pltpu
from jax.sharding import PartitionSpec as P

D = 1536
HEADS = 12
HEAD = 128
TILE = 64
KT = 6
PATCHES = 3
TPP = 2
TPD = 6
ROWS = TPP * TILE
PAIR = 2 * HEAD
BLOCKS = 8
SKEW = 1
EPSILON = 1e-06
SCALE = math.log2(math.e) / math.sqrt(HEAD)
AXES = ("segment", "seq")
VMEM = pl.BlockSpec(memory_space=pltpu.VMEM)
SMEM = pl.BlockSpec(memory_space=pltpu.SMEM)


def head_normed(projected, gain):
    parts = []
    for h in range(projected.shape[1] // HEAD):
        head = projected[:, h * HEAD : (h + 1) * HEAD]
        mean = jnp.mean(head * head, axis=-1, keepdims=True)
        parts.append((head * lax.rsqrt(mean + EPSILON) * gain).astype(jnp.bfloat16))
    return jnp.concatenate(parts, axis=1)


def round_kernel(
    slot,
    with_latent,
    mask_ref,
    gain_q_ref,
    gain_k_ref,
    weights_ref,
    own_ref,
    behind_ref,
    ahead_ref,
    keys_in,
    values_in,
    result_in,
    *rest,
):
    if with_latent:
        latent_ref, *rest = rest
    leaving_ref, keys_ref, values_ref, result_ref, inputs, attended, listed = rest
    block = lax.axis_index("segment")
    frame = lax.axis_index("seq")
    patch = slot - SKEW * block

    @pl.when((patch >= 0) & (patch < PATCHES))
    def _():
        for f, received in enumerate((behind_ref, own_ref, ahead_ref)):
            rows = pl.ds(f * ROWS, ROWS)
            if with_latent:

                @pl.when(block == 0)
                def _(f=f, rows=rows):
                    inputs[rows, :] = latent_ref[f]

                @pl.when(block != 0)
                def _(received=received, rows=rows):
                    inputs[rows, :] = received[...]
            else:
                inputs[rows, :] = received[...]
        lists = []
        slot_of = lax.broadcasted_iota(jnp.int32, (TILE, KT * TILE), 1) // TILE
        for i in range(TPP):
            entries = []
            usable = jnp.zeros((TILE, KT * TILE), jnp.float32)
            for m in range(KT):
                tile = mask_ref[patch * TPP + i, m]
                entries.append(jnp.where(tile >= 0, tile - (frame - 1) * TPD, 0))
                here = jnp.where(tile >= 0, 1.0, 0.0)
                usable = jnp.where(slot_of == m, here, usable)
            lists.append(entries)
            listed[i] = usable

        def weight(j, columns):
            return weights_ref[:, j, :, columns].reshape(D, PAIR)

        def dot(a, b):
            return jnp.dot(a, b, preferred_element_type=jnp.float32)

        def head_pair(c, carry):
            columns = pl.ds(pl.multiple_of(c * PAIR, PAIR), PAIR)
            fresh_k = head_normed(dot(inputs[...], weight(1, columns)), gain_k_ref[...])
            fresh_v = dot(inputs[...], weight(2, columns)).astype(jnp.bfloat16)
            fresh_q = head_normed(dot(inputs[pl.ds(ROWS, ROWS), :], weight(0, columns)), gain_q_ref[...])
            for f in range(3):
                rows = slice(f * ROWS, (f + 1) * ROWS)
                tiles = pl.ds(f * TPD + patch * TPP, TPP)
                keys_ref[tiles, :, columns] = fresh_k[rows].reshape(TPP, TILE, PAIR)
                values_ref[tiles, :, columns] = fresh_v[rows].reshape(TPP, TILE, PAIR)
            for i in range(TPP):
                k = jnp.concatenate([keys_ref[t, :, columns] for t in lists[i]], axis=0)
                v = jnp.concatenate([values_ref[t, :, columns] for t in lists[i]], axis=0)
                outs = []
                for h in range(2):
                    head = slice(h * HEAD, (h + 1) * HEAD)
                    q = fresh_q[i * TILE : (i + 1) * TILE, head]
                    scores = lax.dot_general(
                        q, k[:, head], (((1,), (1,)), ((), ())), preferred_element_type=jnp.float32
                    )
                    weights = jnp.where(listed[i] > 0.0, jnp.exp2(scores * SCALE), 0.0)
                    total = jnp.sum(weights, axis=-1, keepdims=True)
                    outs.append(dot(weights.astype(jnp.bfloat16), v[:, head]) / total)
                attended[pl.ds(i * TILE, TILE), columns] = jnp.concatenate(outs, axis=1).astype(jnp.bfloat16)
            return carry

        lax.fori_loop(0, D // PAIR, head_pair, 0, unroll=True)

        def mix(c, carry):
            columns = pl.ds(pl.multiple_of(c * PAIR, PAIR), PAIR)
            mixed = dot(attended[...], weight(3, columns))
            leaving = (inputs[pl.ds(ROWS, ROWS), columns].astype(jnp.float32) + mixed).astype(jnp.bfloat16)
            leaving_ref[:, columns] = leaving
            result_ref[patch, :, columns] = leaving
            return carry

        lax.fori_loop(0, D // PAIR, mix, 0, unroll=True)


def run_round(slot, mask, gain_q, gain_k, weights, own, behind, ahead, keys, values, result, latent):
    with_latent = latent is not None
    operands = [mask, gain_q, gain_k, weights, own, behind, ahead, keys, values, result]
    if with_latent:
        operands.append(latent)
    operands = operands[:1] + [pltpu.with_memory_space_constraint(o, pltpu.VMEM) for o in operands[1:]]
    return pl.pallas_call(
        functools.partial(round_kernel, slot, with_latent),
        out_shape=(
            jax.ShapeDtypeStruct((ROWS, D), jnp.bfloat16),
            jax.ShapeDtypeStruct(keys.shape, keys.dtype),
            jax.ShapeDtypeStruct(values.shape, values.dtype),
            jax.ShapeDtypeStruct(result.shape, result.dtype),
        ),
        in_specs=[SMEM] + [VMEM] * (len(operands) - 1),
        out_specs=(VMEM,) * 4,
        input_output_aliases={7: 1, 8: 2, 9: 3},
        scratch_shapes=[
            pltpu.VMEM((3 * ROWS, D), jnp.bfloat16),
            pltpu.VMEM((ROWS, D), jnp.bfloat16),
            pltpu.VMEM((TPP, TILE, KT * TILE), jnp.float32),
        ],
        compiler_params=pltpu.CompilerParams(vmem_limit_bytes=16 << 20),
        name="round",
    )(*operands)


def device_of(block, frame, frames):
    return block * frames + frame


def per_device(
    latent,
    stale_kv,
    query_weight,
    key_weight,
    value_weight,
    out_weight,
    query_gain,
    key_gain,
    tile_mask,
):
    frames = lax.axis_size("seq")

    def send(value, blocks, hop, by):
        pairs = [
            (device_of(b, t, frames), device_of(b + hop, t + by, frames))
            for b in blocks
            for t in range(frames)
            if 0 <= t + by < frames
        ]
        return lax.ppermute(value, AXES, pairs)

    everyone = range(BLOCKS)
    shard = jnp.concatenate([query_weight, key_weight, value_weight, out_weight], axis=0)
    weights = lax.all_gather(shard, "seq", axis=0)

    latent3 = jnp.stack([send(latent, [0], 0, 1), latent, send(latent, [0], 0, -1)])
    latent3 = latent3.reshape(3, PATCHES, ROWS, D)
    local = stale_kv[0]
    late = local[:, ROWS:]
    unread = jnp.zeros((2, ROWS, D), jnp.bfloat16)
    window = jnp.stack(
        [
            jnp.concatenate([unread, send(late, everyone, 0, 1)], axis=1),
            local,
            jnp.concatenate([unread, send(late, everyone, 0, -1)], axis=1),
        ],
        axis=1,
    ).reshape(2, 3 * TPD, TILE, D)
    keys, values = window[0], window[1]
    result = jnp.zeros((PATCHES, ROWS, D), jnp.bfloat16)
    empty = jnp.zeros((ROWS, D), jnp.bfloat16)

    last = SKEW * (BLOCKS - 1) + PATCHES - 1
    arrived = {s: (empty, empty, empty) for s in range(SKEW)}
    for slot in range(last + 1):
        own, behind, ahead = arrived[slot]
        leaving, keys, values, result = run_round(
            slot,
            tile_mask,
            query_gain,
            key_gain,
            weights,
            own,
            behind,
            ahead,
            keys,
            values,
            result,
            latent3[:, slot] if slot < PATCHES else None,
        )
        blocks = [b for b in range(BLOCKS - 1) if 0 <= slot - SKEW * b < PATCHES]
        if blocks:
            arrived[slot + SKEW] = tuple(send(leaving, blocks, 1, by) for by in (0, 1, -1))
    return result.reshape(1, PATCHES * ROWS, D)


def solution(mesh):
    return jax.shard_map(
        per_device,
        mesh=mesh,
        in_specs=(
            P("seq", None),
            P("segment", None, "seq", None),
            P("segment", "seq", None),
            P("segment", "seq", None),
            P("segment", "seq", None),
            P("segment", "seq", None),
            P("segment", None),
            P("segment", None),
            P("seq", None),
        ),
        out_specs=P("segment", "seq", None),
        check_vma=False,
    )
```

```python
import functools
import math

import jax
import jax.numpy as jnp
from jax import lax
from jax.experimental import pallas as pl
from jax.experimental.pallas import tpu as pltpu
from jax.sharding import PartitionSpec as P

D = 1536
HEADS = 12
HEAD = 128
TILE = 64
KT = 6
PATCHES = 3
TPP = 2
TPD = 6
ROWS = TPP * TILE
PAIR = 2 * HEAD
BLOCKS = 8
LINE = 4
SHARD = 48
SKEW = 1
EPSILON = 1e-06
SCALE = math.log2(math.e) / math.sqrt(HEAD)
AXES = ("segment", "seq")
VMEM = pl.BlockSpec(memory_space=pltpu.VMEM)
SMEM = pl.BlockSpec(memory_space=pltpu.SMEM)
ANY = pl.BlockSpec(memory_space=pltpu.HBM)
KEY, VALUE, QUERY, OUT = range(4)


def in_vmem(value):
    return pltpu.with_memory_space_constraint(value, pltpu.VMEM)


def head_normed(projected, gain):
    parts = []
    for h in range(projected.shape[1] // HEAD):
        head = projected[:, h * HEAD : (h + 1) * HEAD]
        mean = jnp.mean(head * head, axis=-1, keepdims=True)
        parts.append((head * lax.rsqrt(mean + EPSILON) * gain).astype(jnp.bfloat16))
    return jnp.concatenate(parts, axis=1)


def dot(a, b):
    return jnp.dot(a, b, preferred_element_type=jnp.float32)


def weight(weights_ref, which, columns):
    return weights_ref[:, which, :, columns].reshape(D, PAIR)


def patch_of(slot):
    patch = slot - SKEW * lax.axis_index("segment")
    return patch, (patch >= 0) & (patch < PATCHES)


def own_kernel(slot, with_latent, gain_q_ref, gain_k_ref, weights_ref, own_ref, keys_in, values_in, *rest):
    if with_latent:
        latent_ref, *rest = rest
    keys_ref, values_ref, query_ref, inputs = rest
    patch, active = patch_of(slot)

    @pl.when(active)
    def _():
        if with_latent:
            first = lax.axis_index("segment") == 0

            @pl.when(first)
            def _():
                inputs[...] = latent_ref[1]

            @pl.when(jnp.logical_not(first))
            def _():
                inputs[...] = own_ref[...]
        source = inputs if with_latent else own_ref

        def head_pair(c, carry):
            columns = pl.ds(c * PAIR, PAIR)
            tiles = pl.ds(TPD + patch * TPP, TPP)
            fresh_k = head_normed(dot(source[...], weight(weights_ref, KEY, columns)), gain_k_ref[...])
            fresh_v = dot(source[...], weight(weights_ref, VALUE, columns)).astype(jnp.bfloat16)
            query_ref[:, columns] = head_normed(
                dot(source[...], weight(weights_ref, QUERY, columns)), gain_q_ref[...]
            )
            keys_ref[tiles, :, columns] = fresh_k.reshape(TPP, TILE, PAIR)
            values_ref[tiles, :, columns] = fresh_v.reshape(TPP, TILE, PAIR)
            return carry

        for c in range(D // PAIR):
            head_pair(c, 0)


def rest_kernel(
    slot,
    with_latent,
    mask_ref,
    gain_k_ref,
    weights_ref,
    query_ref,
    own_ref,
    behind_ref,
    ahead_ref,
    keys_in,
    values_in,
    result_in,
    *rest,
):
    if with_latent:
        latent_ref, *rest = rest
    leaving_ref, keys_ref, values_ref, result_ref, inputs, attended, listed = rest
    frame = lax.axis_index("seq")
    patch, active = patch_of(slot)

    @pl.when(active)
    def _():
        for f, received in enumerate((behind_ref, own_ref, ahead_ref)):
            rows = pl.ds(f * ROWS, ROWS)
            if with_latent:
                first = lax.axis_index("segment") == 0

                @pl.when(first)
                def _(f=f, rows=rows):
                    inputs[rows, :] = latent_ref[f]

                @pl.when(jnp.logical_not(first))
                def _(received=received, rows=rows):
                    inputs[rows, :] = received[...]
            else:
                inputs[rows, :] = received[...]
        lists = []
        slot_of = lax.broadcasted_iota(jnp.int32, (TILE, KT * TILE), 1) // TILE
        for i in range(TPP):
            entries = []
            usable = jnp.zeros((TILE, KT * TILE), jnp.float32)
            for m in range(KT):
                tile = mask_ref[patch * TPP + i, m]
                entries.append(jnp.where(tile >= 0, tile - (frame - 1) * TPD, 0))
                here = jnp.where(tile >= 0, 1.0, 0.0)
                usable = jnp.where(slot_of == m, here, usable)
            lists.append(entries)
            listed[i] = usable
        halos = ((0, pl.ds(0, ROWS)), (2, pl.ds(2 * ROWS, ROWS)))
        for c in range(D // PAIR):
            columns = pl.ds(c * PAIR, PAIR)
            sides = jnp.concatenate([inputs[rows, :] for _, rows in halos], axis=0)
            fresh_k = head_normed(dot(sides, weight(weights_ref, KEY, columns)), gain_k_ref[...])
            fresh_v = dot(sides, weight(weights_ref, VALUE, columns)).astype(jnp.bfloat16)
            for n, (f, _) in enumerate(halos):
                rows = slice(n * ROWS, (n + 1) * ROWS)
                tiles = pl.ds(f * TPD + patch * TPP, TPP)
                keys_ref[tiles, :, columns] = fresh_k[rows].reshape(TPP, TILE, PAIR)
                values_ref[tiles, :, columns] = fresh_v[rows].reshape(TPP, TILE, PAIR)
        for c in range(D // PAIR):
            columns = pl.ds(c * PAIR, PAIR)
            for i in range(TPP):
                outs = []
                for h in range(2):
                    at = pl.ds(c * PAIR + h * HEAD, HEAD)
                    k = jnp.concatenate([keys_ref[t, :, at] for t in lists[i]], axis=0)
                    v = jnp.concatenate([values_ref[t, :, at] for t in lists[i]], axis=0)
                    head = slice(None)
                    q = query_ref[pl.ds(i * TILE, TILE), at]
                    scores = lax.dot_general(
                        q, k, (((1,), (1,)), ((), ())), preferred_element_type=jnp.float32
                    )
                    weights = jnp.where(listed[i] > 0.0, jnp.exp2(scores * SCALE), 0.0)
                    total = jnp.sum(weights, axis=-1, keepdims=True)
                    outs.append(dot(weights.astype(jnp.bfloat16), v[:, head]) / total)
                attended[pl.ds(i * TILE, TILE), columns] = jnp.concatenate(outs, axis=1).astype(jnp.bfloat16)
        for c in range(D // PAIR):
            columns = pl.ds(c * PAIR, PAIR)
            mixed = dot(attended[...], weight(weights_ref, OUT, columns))
            leaving = (inputs[pl.ds(ROWS, ROWS), columns].astype(jnp.float32) + mixed).astype(jnp.bfloat16)
            leaving_ref[:, columns] = leaving
            result_ref[patch, :, columns] = leaving


def like(value):
    return jax.ShapeDtypeStruct(value.shape, value.dtype)


def run_own(slot, gain_q, gain_k, weights, own, keys, values, latent):
    operands = [gain_q, gain_k, weights, own, keys, values]
    if latent is not None:
        operands.append(latent)
    operands = [in_vmem(o) for o in operands]
    return pl.pallas_call(
        functools.partial(own_kernel, slot, latent is not None),
        out_shape=(like(keys), like(values), jax.ShapeDtypeStruct((ROWS, D), jnp.bfloat16)),
        in_specs=[VMEM] * len(operands),
        out_specs=(VMEM,) * 3,
        input_output_aliases={4: 0, 5: 1},
        scratch_shapes=[pltpu.VMEM((ROWS, D), jnp.bfloat16)],
        compiler_params=pltpu.CompilerParams(vmem_limit_bytes=8 << 20),
        cost_estimate=pl.CostEstimate(flops=6 * ROWS * D * D, bytes_accessed=0, transcendentals=0),
        name="own",
    )(*operands)


def run_rest(slot, mask, gain_k, weights, query, own, behind, ahead, keys, values, result, latent):
    operands = [gain_k, weights, query, own, behind, ahead, keys, values, result]
    if latent is not None:
        operands.append(latent)
    operands = [mask] + [in_vmem(o) for o in operands]
    return pl.pallas_call(
        functools.partial(rest_kernel, slot, latent is not None),
        out_shape=(jax.ShapeDtypeStruct((ROWS, D), jnp.bfloat16), like(keys), like(values), like(result)),
        in_specs=[SMEM] + [VMEM] * (len(operands) - 1),
        out_specs=(VMEM,) * 4,
        input_output_aliases={7: 1, 8: 2, 9: 3},
        scratch_shapes=[
            pltpu.VMEM((3 * ROWS, D), jnp.bfloat16),
            pltpu.VMEM((ROWS, D), jnp.bfloat16),
            pltpu.VMEM((TPP, TILE, KT * TILE), jnp.float32),
        ],
        compiler_params=pltpu.CompilerParams(vmem_limit_bytes=16 << 20),
        cost_estimate=pl.CostEstimate(flops=14 * ROWS * D * D, bytes_accessed=0, transcendentals=0),
        name="rest",
    )(*operands)


def run_round(slot, mask, gain_q, gain_k, weights, own, behind, ahead, keys, values, result, latent):
    keys, values, query = run_own(slot, gain_q, gain_k, weights, own, keys, values, latent)
    return run_rest(slot, mask, gain_k, weights, query, own, behind, ahead, keys, values, result, latent)


def together(*values):
    return lax.optimization_barrier(values)


def assemble_kernel(plan, lines, n_pieces, *refs):
    pieces, rest = refs[:n_pieces], refs[n_pieces:]
    weights_ref, sem = rest[-2:]
    frame = lax.axis_index("seq")
    z, y = frame // LINE, frame % LINE
    copies = []
    for piece, place, dz, dy, first in plan:
        source = lax.rem(z + dz + lines, lines) * LINE + lax.rem(y + dy + LINE, LINE)
        copies.append(
            pltpu.make_async_copy(
                pieces[piece].at[place], weights_ref.at[source, pl.ds(first, 2)], sem.at[len(copies)]
            )
        )
    for copy in copies:
        copy.start()
    for copy in copies:
        copy.wait()


def assemble(plan, pieces, lines, former):
    operands = [pltpu.with_memory_space_constraint(p, pltpu.HBM) for p in pieces]
    aliases = {}
    if former is not None:
        aliases = {len(operands): 0}
        operands.append(in_vmem(former))
    return pl.pallas_call(
        functools.partial(assemble_kernel, plan, lines, len(pieces)),
        out_shape=jax.ShapeDtypeStruct((lines * LINE, 4, SHARD, D), jnp.bfloat16),
        in_specs=[ANY] * len(pieces) + [VMEM] * (former is not None),
        out_specs=VMEM,
        input_output_aliases=aliases,
        scratch_shapes=[pltpu.SemaphoreType.DMA((len(plan),))],
        compiler_params=pltpu.CompilerParams(vmem_limit_bytes=2 << 20),
        cost_estimate=pl.CostEstimate(flops=0, bytes_accessed=sum(p.size * 4 for p in pieces), transcendentals=0),
        name="assemble",
    )(*operands)


def per_device(
    latent,
    stale_kv,
    query_weight,
    key_weight,
    value_weight,
    out_weight,
    query_gain,
    key_gain,
    tile_mask,
):
    frames = lax.axis_size("seq")
    lines = frames // LINE

    def send(value, blocks, hop, by):
        pairs = [
            (b * frames + t, (b + hop) * frames + t + by)
            for b in blocks
            for t in range(frames)
            if 0 <= t + by < frames
        ]
        return lax.ppermute(value, AXES, pairs)

    def shift_y(value, by):
        return lax.ppermute(value, "seq", [(t, t // LINE * LINE + (t + by) % LINE) for t in range(frames)])

    def shift_z(value, by):
        return lax.ppermute(value, "seq", [(t, (t + LINE * by) % frames) for t in range(frames)])

    everyone = range(BLOCKS)
    first = jnp.concatenate([key_weight, value_weight], axis=0)
    second = jnp.concatenate([query_weight, out_weight], axis=0)
    local = stale_kv[0]
    late = local[:, ROWS:]

    y_up, y_down = shift_y(first, 1), shift_y(first, -1)
    z_up, z_down = [second], [second]
    z_up.append(shift_z(second, 1))
    z_down.append(shift_z(second, -1))
    y_up, y_down, z_up[1], z_down[1] = together(y_up, y_down, z_up[1], z_down[1])
    y_far = [shift_y(y_up[:1], 1), shift_y(y_down[1:], -1)]
    z_up.append(shift_z(z_up[1], 1))
    z_down.append(shift_z(z_down[1], -1))
    y_far[0], y_far[1], z_up[2], z_down[2], late = together(y_far[0], y_far[1], z_up[2], z_down[2], late)
    row = jnp.stack([first, y_up, y_down, jnp.concatenate(y_far, axis=0)])
    row_places = (0, -1, 1, 2)
    z_up.append(shift_z(z_up[2], 1))
    z_down.append(shift_z(z_down[2], -1))
    rows_up, rows_down = [row, shift_z(row, 1)], [row, shift_z(row, -1)]
    stale_behind, stale_ahead = send(late, everyone, 0, 1), send(late, everyone, 0, -1)
    z_far = [shift_z(z_up[3][:1], 1), shift_z(z_down[3][1:], -1)]
    column = jnp.stack(z_up + z_down[1:] + [jnp.concatenate(z_far, axis=0)])
    column_places = (0, -1, -2, -3, 1, 2, 3, 4)
    columns_up, columns_down = shift_y(column, 1), shift_y(column, -1)
    for _ in range(2):
        rows_up.append(shift_z(rows_up[-1], 1))
        rows_down.append(shift_z(rows_down[-1], -1))
    half = LINE // 2
    row_far = [shift_z(rows_up[-1][:half], 1), shift_z(rows_down[-1][half:], -1)]
    half = lines // 2
    column_far = [shift_y(columns_up[:half], 1), shift_y(columns_down[half:], -1)]
    latent_behind, latent_ahead = send(latent, [0], 0, 1), send(latent, [0], 0, -1)

    stages = ([], []), ([], [])

    def place(stage, array, dzs, dys, which):
        pieces, plan = stages[stage]
        for n in range(array.shape[0]):
            plan.append((len(pieces), n, dzs[n % len(dzs)], dys[n % len(dys)], 2 * which))
        pieces.append(array)

    place(0, row, (0,), row_places, 0)
    for n in range(1, len(rows_up)):
        place(0, rows_up[n], (-n,), row_places, 0)
        place(0, rows_down[n], (n,), row_places, 0)
    place(1, row_far[0], (len(rows_up),), row_places[: LINE // 2], 0)
    place(1, row_far[1], (len(rows_up),), row_places[LINE // 2 :], 0)
    place(0, column, column_places, (0,), 1)
    place(0, columns_up, column_places, (-1,), 1)
    place(0, columns_down, column_places, (1,), 1)
    place(1, column_far[0], column_places[:half], (2,), 1)
    place(1, column_far[1], column_places[half:], (2,), 1)
    weights = None
    for pieces, plan in stages:
        weights = assemble(plan, pieces, lines, weights)
    latent3 = jnp.stack([latent_behind, latent, latent_ahead]).reshape(3, PATCHES, ROWS, D)
    unread = jnp.zeros((2, ROWS, D), jnp.bfloat16)
    window = jnp.stack(
        [
            jnp.concatenate([unread, stale_behind], axis=1),
            local,
            jnp.concatenate([unread, stale_ahead], axis=1),
        ],
        axis=1,
    ).reshape(2, 3 * TPD, TILE, D)
    keys, values = window[0], window[1]
    result = jnp.zeros((PATCHES, ROWS, D), jnp.bfloat16)
    empty = jnp.zeros((ROWS, D), jnp.bfloat16)

    last = SKEW * (BLOCKS - 1) + PATCHES - 1
    arrived = {s: (empty, empty, empty) for s in range(SKEW)}
    for slot in range(last + 1):
        own, behind, ahead = arrived[slot]
        leaving, keys, values, result = run_round(
            slot,
            tile_mask,
            query_gain,
            key_gain,
            weights,
            own,
            behind,
            ahead,
            keys,
            values,
            result,
            latent3[:, slot] if slot < PATCHES else None,
        )
        blocks = [b for b in range(BLOCKS - 1) if 0 <= slot - SKEW * b < PATCHES]
        if slot + SKEW <= last:
            arrived[slot + SKEW] = tuple(send(leaving, blocks, 1, by) for by in (0, 1, -1))
    return result.reshape(1, PATCHES * ROWS, D)


def solution(mesh):
    return jax.shard_map(
        per_device,
        mesh=mesh,
        in_specs=(
            P("seq", None),
            P("segment", None, "seq", None),
            P("segment", "seq", None),
            P("segment", "seq", None),
            P("segment", "seq", None),
            P("segment", "seq", None),
            P("segment", None),
            P("segment", None),
            P("seq", None),
        ),
        out_specs=P("segment", "seq", None),
        check_vma=False,
    )
```

```python
import functools
import math

import jax
import jax.numpy as jnp
from jax import lax
from jax.experimental import pallas as pl
from jax.experimental.pallas import tpu as pltpu
from jax.sharding import PartitionSpec as P

D = 1536
HEADS = 12
HEAD = 128
TILE = 64
KT = 6
PATCHES = 3
TPP = 2
TPD = 6
ROWS = TPP * TILE
PAIR = 2 * HEAD
BLOCKS = 8
SKEW = 1
EPSILON = 1e-06
SCALE = math.log2(math.e) / math.sqrt(HEAD)
AXES = ("segment", "seq")
VMEM = pl.BlockSpec(memory_space=pltpu.VMEM)
SMEM = pl.BlockSpec(memory_space=pltpu.SMEM)


def head_normed(projected, gain):
    parts = []
    for h in range(projected.shape[1] // HEAD):
        head = projected[:, h * HEAD : (h + 1) * HEAD]
        mean = jnp.mean(head * head, axis=-1, keepdims=True)
        parts.append((head * lax.rsqrt(mean + EPSILON) * gain).astype(jnp.bfloat16))
    return jnp.concatenate(parts, axis=1)


def round_kernel(
    slot,
    with_latent,
    mask_ref,
    gain_q_ref,
    gain_k_ref,
    weights_ref,
    own_ref,
    behind_ref,
    ahead_ref,
    keys_in,
    values_in,
    result_in,
    *rest,
):
    if with_latent:
        latent_ref, *rest = rest
    leaving_ref, keys_ref, values_ref, result_ref, inputs, attended, listed = rest
    block = lax.axis_index("segment")
    frame = lax.axis_index("seq")
    patch = slot - SKEW * block

    @pl.when((patch >= 0) & (patch < PATCHES))
    def _():
        for f, received in enumerate((behind_ref, own_ref, ahead_ref)):
            rows = pl.ds(f * ROWS, ROWS)
            if with_latent:

                @pl.when(block == 0)
                def _(f=f, rows=rows):
                    inputs[rows, :] = latent_ref[f]

                @pl.when(block != 0)
                def _(received=received, rows=rows):
                    inputs[rows, :] = received[...]
            else:
                inputs[rows, :] = received[...]
        lists = []
        slot_of = lax.broadcasted_iota(jnp.int32, (TILE, KT * TILE), 1) // TILE
        for i in range(TPP):
            entries = []
            usable = jnp.zeros((TILE, KT * TILE), jnp.float32)
            for m in range(KT):
                tile = mask_ref[patch * TPP + i, m]
                entries.append(jnp.where(tile >= 0, tile - (frame - 1) * TPD, 0))
                here = jnp.where(tile >= 0, 1.0, 0.0)
                usable = jnp.where(slot_of == m, here, usable)
            lists.append(entries)
            listed[i] = usable

        def weight(j, columns):
            return weights_ref[:, j, :, columns].reshape(D, PAIR)

        def dot(a, b):
            return jnp.dot(a, b, preferred_element_type=jnp.float32)

        def head_pair(c, carry):
            columns = pl.ds(pl.multiple_of(c * PAIR, PAIR), PAIR)
            fresh_k = head_normed(dot(inputs[...], weight(1, columns)), gain_k_ref[...])
            fresh_v = dot(inputs[...], weight(2, columns)).astype(jnp.bfloat16)
            fresh_q = head_normed(dot(inputs[pl.ds(ROWS, ROWS), :], weight(0, columns)), gain_q_ref[...])
            for f in range(3):
                rows = slice(f * ROWS, (f + 1) * ROWS)
                tiles = pl.ds(f * TPD + patch * TPP, TPP)
                keys_ref[tiles, :, columns] = fresh_k[rows].reshape(TPP, TILE, PAIR)
                values_ref[tiles, :, columns] = fresh_v[rows].reshape(TPP, TILE, PAIR)
            attended[:, columns] = fresh_q
            return carry

        lax.fori_loop(0, D // PAIR, head_pair, 0, unroll=True)

        def attend_pair(c, carry):
            columns = pl.ds(pl.multiple_of(c * PAIR, PAIR), PAIR)
            for i in range(TPP):
                k = jnp.concatenate([keys_ref[t, :, columns] for t in lists[i]], axis=0)
                v = jnp.concatenate([values_ref[t, :, columns] for t in lists[i]], axis=0)
                queries = attended[pl.ds(i * TILE, TILE), columns]
                outs = []
                for h in range(2):
                    head = slice(h * HEAD, (h + 1) * HEAD)
                    q = queries[:, head]
                    scores = lax.dot_general(
                        q, k[:, head], (((1,), (1,)), ((), ())), preferred_element_type=jnp.float32
                    )
                    weights = jnp.where(listed[i] > 0.0, jnp.exp2(scores * SCALE), 0.0)
                    total = jnp.sum(weights, axis=-1, keepdims=True)
                    outs.append(dot(weights.astype(jnp.bfloat16), v[:, head]) / total)
                attended[pl.ds(i * TILE, TILE), columns] = jnp.concatenate(outs, axis=1).astype(jnp.bfloat16)
            return carry

        lax.fori_loop(0, D // PAIR, attend_pair, 0, unroll=True)

        def mix(c, carry):
            columns = pl.ds(pl.multiple_of(c * PAIR, PAIR), PAIR)
            mixed = dot(attended[...], weight(3, columns))
            leaving = (inputs[pl.ds(ROWS, ROWS), columns].astype(jnp.float32) + mixed).astype(jnp.bfloat16)
            leaving_ref[:, columns] = leaving
            result_ref[patch, :, columns] = leaving
            return carry

        lax.fori_loop(0, D // PAIR, mix, 0, unroll=True)


def run_round(slot, mask, gain_q, gain_k, weights, own, behind, ahead, keys, values, result, latent):
    with_latent = latent is not None
    operands = [mask, gain_q, gain_k, weights, own, behind, ahead, keys, values, result]
    if with_latent:
        operands.append(latent)
    operands = operands[:1] + [pltpu.with_memory_space_constraint(o, pltpu.VMEM) for o in operands[1:]]
    return pl.pallas_call(
        functools.partial(round_kernel, slot, with_latent),
        out_shape=(
            jax.ShapeDtypeStruct((ROWS, D), jnp.bfloat16),
            jax.ShapeDtypeStruct(keys.shape, keys.dtype),
            jax.ShapeDtypeStruct(values.shape, values.dtype),
            jax.ShapeDtypeStruct(result.shape, result.dtype),
        ),
        in_specs=[SMEM] + [VMEM] * (len(operands) - 1),
        out_specs=(VMEM,) * 4,
        input_output_aliases={7: 1, 8: 2, 9: 3},
        scratch_shapes=[
            pltpu.VMEM((3 * ROWS, D), jnp.bfloat16),
            pltpu.VMEM((ROWS, D), jnp.bfloat16),
            pltpu.VMEM((TPP, TILE, KT * TILE), jnp.float32),
        ],
        compiler_params=pltpu.CompilerParams(vmem_limit_bytes=16 << 20),
        name="round",
    )(*operands)


def device_of(block, frame, frames):
    return block * frames + frame


def per_device(
    latent,
    stale_kv,
    query_weight,
    key_weight,
    value_weight,
    out_weight,
    query_gain,
    key_gain,
    tile_mask,
):
    frames = lax.axis_size("seq")

    def send(value, blocks, hop, by):
        pairs = [
            (device_of(b, t, frames), device_of(b + hop, t + by, frames))
            for b in blocks
            for t in range(frames)
            if 0 <= t + by < frames
        ]
        return lax.ppermute(value, AXES, pairs)

    everyone = range(BLOCKS)
    shard = jnp.concatenate([query_weight, key_weight, value_weight, out_weight], axis=0)
    weights = lax.all_gather(shard, "seq", axis=0)

    latent3 = jnp.stack([send(latent, [0], 0, 1), latent, send(latent, [0], 0, -1)])
    latent3 = latent3.reshape(3, PATCHES, ROWS, D)
    local = stale_kv[0]
    late = local[:, ROWS:]
    unread = jnp.zeros((2, ROWS, D), jnp.bfloat16)
    window = jnp.stack(
        [
            jnp.concatenate([unread, send(late, everyone, 0, 1)], axis=1),
            local,
            jnp.concatenate([unread, send(late, everyone, 0, -1)], axis=1),
        ],
        axis=1,
    ).reshape(2, 3 * TPD, TILE, D)
    keys, values = window[0], window[1]
    result = jnp.zeros((PATCHES, ROWS, D), jnp.bfloat16)
    empty = jnp.zeros((ROWS, D), jnp.bfloat16)

    last = SKEW * (BLOCKS - 1) + PATCHES - 1
    arrived = {s: (empty, empty, empty) for s in range(SKEW)}
    for slot in range(last + 1):
        own, behind, ahead = arrived[slot]
        leaving, keys, values, result = run_round(
            slot,
            tile_mask,
            query_gain,
            key_gain,
            weights,
            own,
            behind,
            ahead,
            keys,
            values,
            result,
            latent3[:, slot] if slot < PATCHES else None,
        )
        blocks = [b for b in range(BLOCKS - 1) if 0 <= slot - SKEW * b < PATCHES]
        if blocks:
            arrived[slot + SKEW] = tuple(send(leaving, blocks, 1, by) for by in (0, 1, -1))
    return result.reshape(1, PATCHES * ROWS, D)


def solution(mesh):
    return jax.shard_map(
        per_device,
        mesh=mesh,
        in_specs=(
            P("seq", None),
            P("segment", None, "seq", None),
            P("segment", "seq", None),
            P("segment", "seq", None),
            P("segment", "seq", None),
            P("segment", "seq", None),
            P("segment", None),
            P("segment", None),
            P("seq", None),
        ),
        out_specs=P("segment", "seq", None),
        check_vma=False,
    )
```
